32 devices in a mesh: ctx: 8 (over y, x, core), tp: 4 (over z).
Axes of the slice: x: 2, y: 2, z: 4, core: 2. Of those that a mesh axis runs over, the one named last changes fastest.
Arguments:
- hidden: bfloat16 [8192, 4096], P('ctx'), may hold values from -6 to 6
- norm_gain: float32 [4096], replicated, may hold values from 0.25 to 1.75
- w_query: bfloat16 [4096, 4096], P(None, 'tp')
- w_key: bfloat16 [4096, 1024], P(None, 'tp')
- w_value: bfloat16 [4096, 1024], P(None, 'tp'), may hold values from -0.09375 to 0.09375
- w_output: bfloat16 [4096, 4096], P('tp'), may hold values from -0.09375 to 0.09375
- positions: int32 [4096], P('ctx'), may hold values from -1 to 8191, as said below
- counts: int32 [32], P('ctx'), may hold values from 1 to 128, as said below
- router_weight: float32 [8192], P('ctx'), may hold values from 0.25 to 2
Outputs:
- mixed: bfloat16 [8192, 4096], P('ctx', 'tp')
The draws below stay inside these ranges and needn't reach their ends.
Inputs may be any that keep to these rules, and one draw needn't show every extreme that they name: Slots of ctx index s are those from s * 512 to (s + 1) * 512 - 1; their live slots hold distinct positions from s * 1024 to (s + 1) * 1024 - 1, increasing in slot order; other slots hold -1. `counts`: blocks of ctx index s are those from s * 4 to (s + 1) * 4 - 1; one block among all 32 is full.
All inputs are finite; a program needn't handle non-finite values.
Results may differ from the reference program's by a relative error of at most 0.0089.
Values may be sent and summed in bfloat16 or wider, within the bound.
No kernel may reach another device: no remote copies, remote signals or barrier semaphores. Data moves between devices by JAX's collectives and lax.ppermute only.
A program may use at most 128 MiB of HBM per device.

```python
import math
import jax
import jax.numpy as jnp
from jax import lax

D = 4096
HEADS = 32
KV_HEADS = 8
HEAD_DIM = 128
BLOCK = 128
SEQ_DEV = 1024
CAP = 512
LENGTH = 8192
N_CTX = 8
N_TP = 4


def routed_layout(key):
    base = jax.random.fold_in(key, 31)
    blocks = CAP // BLOCK
    level = jax.random.randint(jax.random.fold_in(base, 1), (N_CTX, 1), 1, 5)
    lowest = jnp.maximum(1, BLOCK * level // 8)
    highest = BLOCK * level // 4 + 1
    raw = jax.random.randint(jax.random.fold_in(base, 2), (N_CTX, blocks), 0, 2 ** 20)
    counts = lowest + raw % (highest - lowest)
    full_shard = jax.random.randint(jax.random.fold_in(base, 4), (), 0, N_CTX)
    full_block = jax.random.randint(jax.random.fold_in(base, 5), (), 0, blocks)
    pick = (jnp.arange(N_CTX)[:, None] == full_shard) & (jnp.arange(blocks)[None, :] == full_block)
    counts = jnp.where(pick, BLOCK, counts).astype(jnp.int32)
    totals = jnp.sum(counts, axis=1)
    shard_keys = jax.random.split(jax.random.fold_in(base, 3), N_CTX)
    orders = jax.vmap(lambda item: jax.random.permutation(item, SEQ_DEV))(shard_keys)[:, :CAP]
    chosen = jnp.where(jnp.arange(CAP)[None, :] < totals[:, None], orders, SEQ_DEV)
    ordered = jnp.sort(chosen, axis=1)
    starts = jnp.cumsum(counts, axis=1) - counts
    inner = jnp.arange(BLOCK)
    wanted = (starts[:, :, None] + inner[None, None, :]).reshape(N_CTX, CAP)
    taken = jnp.take_along_axis(ordered, jnp.minimum(wanted, CAP - 1), axis=1)
    live = (inner[None, None, :] < counts[:, :, None]).reshape(N_CTX, CAP)
    placed = taken + jnp.arange(N_CTX)[:, None] * SEQ_DEV
    positions = jnp.where(live, placed, -1).astype(jnp.int32)
    return (counts.reshape(-1), positions.reshape(-1))


def query_weights(key):
    return jax.random.normal(jax.random.fold_in(key, 11), (D, HEADS * HEAD_DIM), jnp.float32) * D ** (-0.5)


def draw_positions(key, part):
    return routed_layout(key)[1]


def draw_counts(key, part):
    return routed_layout(key)[0]


def draw_w_query(key, part):
    return query_weights(key).astype(jnp.bfloat16)


def draw_w_key(key, part):
    noise = jax.random.normal(jax.random.fold_in(key, 12), (D, KV_HEADS * HEAD_DIM), jnp.float32) * D ** (-0.5)
    return noise.astype(jnp.bfloat16)


def shard_levels(rng, extent, shards, least, top_value):
    gain, own = 1.0, jax.random.fold_in(rng, 6)
    for axis_at, shards_of in shards:
        steps = jnp.exp(jax.random.uniform(jax.random.fold_in(own, axis_at), (shards_of,), jnp.float32, least / len(shards), top_value / len(shards)))
        gain = gain * jnp.repeat(steps, extent[axis_at] // shards_of).reshape([-1 if axis == axis_at else 1 for axis in range(len(extent))])
    return gain


def gaussian(own_key, shape, spread, bound, cuts=(), held_as=jnp.bfloat16):
    values = jax.random.normal(own_key, shape, jnp.float32) * spread
    if len(cuts) > 0:
        values = shard_levels(own_key, shape, cuts, -0.22, 0.18) * values
    return jnp.clip(values, min=-bound, max=bound).astype(held_as)


def setup_inputs(seed: int = 0) -> dict:
    seeds = jax.random.split(jax.random.key(seed), 10)
    hidden = gaussian(seeds[0], (LENGTH, D), 1.0, 6.0, ((0, 8),))
    norm_gain = jnp.clip(1.0 + 0.15 * jax.random.normal(seeds[1], (D,), jnp.float32), 0.25, 1.75)
    w_query = draw_w_query(jax.random.fold_in(seeds[9], 71), 0)
    w_key = draw_w_key(jax.random.fold_in(seeds[9], 71), 0)
    w_value = gaussian(seeds[4], (D, KV_HEADS * HEAD_DIM), D ** -0.5, 0.09375, ((1, 4),))
    w_output = gaussian(seeds[5], (HEADS * HEAD_DIM, D), (HEADS * HEAD_DIM) ** -0.5, 0.09375, ((0, 4),))
    positions = draw_positions(jax.random.fold_in(seeds[9], 71), 0)
    counts = draw_counts(jax.random.fold_in(seeds[9], 71), 0)
    router_weight = jnp.clip(jnp.exp(math.log(2.0) - 2.0794415 * jax.random.uniform(seeds[8], (LENGTH,), jnp.float32) ** shard_levels(seeds[8], (LENGTH,), ((0, 8),), -0.2, 0.2)), 0.25, 2.0)
    return {"hidden": hidden, "norm_gain": norm_gain, "w_query": w_query, "w_key": w_key, "w_value": w_value, "w_output": w_output, "positions": positions, "counts": counts, "router_weight": router_weight}


def rotate(field, angle_pos):
    half = field.shape[-1] // 2
    freq = 500000.0 ** (-2.0 * jnp.arange(half, dtype=jnp.float32) / field.shape[-1])
    angle = angle_pos[:, None] * freq[None, :]
    cosine = jnp.cos(angle)[:, None, :]
    sine = jnp.sin(angle)[:, None, :]
    first = field[..., :half]
    second = field[..., half:]
    return jnp.concatenate([first * cosine - second * sine, second * cosine + first * sine], axis=-1)

def reference(hidden, norm_gain, w_query, w_key, w_value, w_output, positions, counts, router_weight):
    slot_count = positions.shape[0]
    within = jnp.arange(slot_count, dtype=jnp.int32)
    block_of = (within // BLOCK).astype(jnp.int32)
    live = within % BLOCK < counts[block_of]
    index = jnp.where(live, positions, 0).astype(jnp.int32)
    rows = hidden[index].astype(jnp.float32) * live[:, None].astype(jnp.float32)
    scale_rows = lax.rsqrt(lax.optimization_barrier(jnp.mean(rows * rows, axis=-1, keepdims=True)) + 1e-05)
    normed = (rows * scale_rows * norm_gain[None, :]).astype(jnp.bfloat16)
    queries = jnp.dot(normed, w_query, preferred_element_type=jnp.float32)
    key_rows = jnp.dot(normed, w_key, preferred_element_type=jnp.float32)
    value_rows = jnp.dot(normed, w_value, preferred_element_type=jnp.float32).astype(jnp.bfloat16)
    angle_pos = index.astype(jnp.float32)
    queries = rotate(queries.reshape(slot_count, HEADS, HEAD_DIM), angle_pos).astype(jnp.bfloat16)
    key_rows = rotate(key_rows.reshape(slot_count, KV_HEADS, HEAD_DIM), angle_pos).astype(jnp.bfloat16)
    value_rows = value_rows.reshape(slot_count, KV_HEADS, HEAD_DIM)
    query_pos = jnp.where(live, positions, -1)
    key_pos = jnp.where(live, positions, 2 ** 30)
    allowed = key_pos[None, :] <= query_pos[:, None]
    group = HEADS // KV_HEADS

    def one_head(head):
        query_head = queries[:, head, :]
        key_head = key_rows[:, head // group, :]
        value_head = value_rows[:, head // group, :]
        score = jnp.dot(query_head, key_head.T, preferred_element_type=jnp.float32) * HEAD_DIM ** (-0.5)
        masked = jnp.where(allowed, score, -1e+30)
        largest = lax.optimization_barrier(jnp.max(masked, axis=-1, keepdims=True))
        weight = jnp.where(allowed, jnp.exp(masked - largest), 0.0)
        total = lax.optimization_barrier(jnp.sum(weight, axis=-1, keepdims=True))
        total = jnp.where(total > 0, total, 1.0)
        product = jnp.dot(weight.astype(jnp.bfloat16), value_head, preferred_element_type=jnp.float32)
        return (product / total).astype(jnp.bfloat16)
    heads_out = lax.map(one_head, jnp.arange(HEADS, dtype=jnp.int32))
    attn = jnp.transpose(heads_out, (1, 0, 2)).reshape(slot_count, HEADS * HEAD_DIM)
    width = HEADS * HEAD_DIM // N_TP
    attn_groups = attn.reshape(slot_count, N_TP, width)
    output_groups = w_output.reshape(N_TP, width, w_output.shape[1])

    def add_group(carry, member):
        product = jnp.dot(attn_groups[:, member, :], output_groups[member], preferred_element_type=jnp.float32)
        return (carry + product.astype(jnp.bfloat16).astype(jnp.float32), None)
    proj, unused = lax.scan(add_group, jnp.zeros((slot_count, w_output.shape[1]), jnp.float32), jnp.arange(N_TP, dtype=jnp.int32))
    target = jnp.where(live, positions, hidden.shape[0]).astype(jnp.int32)
    update = router_weight[index][:, None] * proj
    mixed = hidden.astype(jnp.float32).at[target].add(update, mode='drop')
    return mixed.astype(jnp.bfloat16)
```

```python
import functools

import jax
import jax.numpy as jnp
import numpy as np
from jax import lax
from jax.experimental import pallas as pl
from jax.experimental.pallas import tpu as pltpu
from jax.sharding import PartitionSpec as P

HEAD_DIM = 128
BLOCK = 128
F32 = jnp.float32
BF16 = jnp.bfloat16
NT = (((1,), (1,)), ((), ()))


def freq_rows():
    half = HEAD_DIM // 2
    freq = 500000.0 ** (-2.0 * np.arange(half, dtype=np.float64) / HEAD_DIM)
    return np.concatenate([freq, freq]).astype(np.float32).reshape(1, HEAD_DIM)


def rope(field, cosine, sine):
    return field * cosine + pltpu.roll(field, HEAD_DIM // 2, 1) * sine


def prepare(
    counts_ref,
    base_ref,
    pos_ref,
    freq_ref,
    gain_ref,
    router_ref,
    hidden_ref,
    key_hbm,
    value_hbm,
    payload_ref,
    normed_ref,
    aux_ref,
    select,
    square,
    key_w,
    value_w,
    sems,
):
    step = pl.program_id(0)
    steps = pl.num_programs(0)
    rows = normed_ref.shape[0]
    depth = normed_ref.shape[1]
    tile = hidden_ref.shape[1]
    seq = hidden_ref.shape[0]
    blocks = counts_ref.shape[0]
    load_key = pltpu.make_async_copy(key_hbm, key_w, sems.at[0])
    load_value = pltpu.make_async_copy(value_hbm, value_w, sems.at[1])

    @pl.when(step == 0)
    def _():
        load_key.start()
        load_value.start()
        slot = lax.broadcasted_iota(jnp.int32, (1, rows), 1)
        compact = jnp.full((1, rows), -1, jnp.int32)
        offset = jnp.int32(0)
        for b in range(blocks):
            count = counts_ref[b]
            inside = (slot >= b * BLOCK) & (slot < b * BLOCK + count)
            compact = jnp.where(inside, slot - b * BLOCK + offset, compact)
            offset = offset + count
        line = lax.broadcasted_iota(jnp.int32, (rows, rows), 0)
        match = line == compact
        pos_col = jnp.sum(
            jnp.where(match, pos_ref[...].astype(F32), 0.0), axis=1, keepdims=True
        )
        live = lax.broadcasted_iota(jnp.int32, (rows, 1), 0) < offset
        local = jnp.where(live, pos_col.astype(jnp.int32) - base_ref[0], -1)
        place = lax.broadcasted_iota(jnp.int32, (rows, seq), 1)
        hit = place == local
        select[...] = jnp.where(hit, 1.0, 0.0).astype(BF16)
        router = jnp.sum(jnp.where(hit, router_ref[...], 0.0), axis=1, keepdims=True)
        angle = pos_col * freq_ref[...]
        sign = jnp.where(
            lax.broadcasted_iota(jnp.int32, (1, HEAD_DIM), 1) < HEAD_DIM // 2, -1.0, 1.0
        )
        aux_ref[:, :HEAD_DIM] = jnp.cos(angle)
        aux_ref[:, HEAD_DIM : 2 * HEAD_DIM] = jnp.sin(angle) * sign
        aux_ref[:, 2 * HEAD_DIM : 3 * HEAD_DIM] = jnp.broadcast_to(
            local.astype(F32), (rows, HEAD_DIM)
        )
        aux_ref[:, 3 * HEAD_DIM :] = jnp.broadcast_to(router, (rows, HEAD_DIM))
        square[...] = jnp.zeros_like(square)

    picked = jnp.dot(select[...], hidden_ref[...], preferred_element_type=F32)
    square[...] += jnp.sum(picked * picked, axis=1, keepdims=True)
    normed_ref[:, pl.ds(pl.multiple_of(step * tile, tile), tile)] = picked.astype(BF16)

    @pl.when(step == steps - 1)
    def _():
        scale = lax.rsqrt(square[...] / depth + 1e-05)

        @pl.loop(0, steps)
        def _(i):
            span = pl.ds(pl.multiple_of(i * tile, tile), tile)
            normed_ref[:, span] = (
                normed_ref[:, span].astype(F32) * scale * gain_ref[:, span]
            ).astype(BF16)

        load_key.wait()
        load_value.wait()
        cosine = aux_ref[:, :HEAD_DIM]
        sine = aux_ref[:, HEAD_DIM : 2 * HEAD_DIM]
        kv_heads = key_w.shape[1] // HEAD_DIM
        keys = jnp.dot(normed_ref[...], key_w[...], preferred_element_type=F32)
        for g in range(kv_heads):
            head = keys[:, g * HEAD_DIM : (g + 1) * HEAD_DIM]
            payload_ref[g * rows : (g + 1) * rows, :] = rope(head, cosine, sine).astype(BF16)
        values = jnp.dot(normed_ref[...], value_w[...], preferred_element_type=F32)
        first = kv_heads * rows
        for c in range(rows // BLOCK):
            for g in range(kv_heads):
                part = values[c * BLOCK : (c + 1) * BLOCK, g * HEAD_DIM : (g + 1) * HEAD_DIM]
                at = first + (c * kv_heads + g) * HEAD_DIM
                payload_ref[at : at + HEAD_DIM, :] = jnp.transpose(part).astype(BF16)


def project_queries(normed_ref, weight_ref, aux_ref, out_ref):
    rows = normed_ref.shape[0]
    fields = jnp.dot(normed_ref[...], weight_ref[...], preferred_element_type=F32)
    cosine = aux_ref[:, :HEAD_DIM]
    sine = aux_ref[:, HEAD_DIM : 2 * HEAD_DIM]
    for h in range(weight_ref.shape[1] // HEAD_DIM):
        turned = rope(fields[:, h * HEAD_DIM : (h + 1) * HEAD_DIM], cosine, sine).astype(BF16)
        for r in range(rows // BLOCK):
            out_ref[r, 0, h * BLOCK : (h + 1) * BLOCK, :] = turned[r * BLOCK : (r + 1) * BLOCK]


def attend(shards, parts, first_block, info_ref, query_ref, *refs):
    payloads = refs[:shards]
    output_hbm = refs[shards]
    outs = refs[shards + 1 : shards + 1 + parts]
    kv, weight, state, top, total, rows_sc, sems, weight_sem = refs[shards + 1 + parts :]
    block = first_block + pl.program_id(0)
    me = info_ref[0]
    kv_heads = query_ref.shape[1]
    columns = query_ref.shape[2]
    group = columns // BLOCK
    chunks = kv.shape[1] // (2 * kv_heads * HEAD_DIM)
    rows = chunks * BLOCK
    factor = HEAD_DIM**-0.5 * 1.4426950408889634
    load_weight = pltpu.make_async_copy(output_hbm, weight, weight_sem)

    def load(k):
        return pltpu.make_async_copy(payloads[k], kv.at[k], sems.at[k])

    def needed(k):
        return lax.bitwise_xor(me, k) < me

    @pl.when(pl.program_id(0) == 0)
    def _():
        load(0).start()
        for k in range(1, shards):
            @pl.when(needed(k))
            def _():
                load(k).start()
        load_weight.start()
        load(0).wait()
        for k in range(1, shards):
            @pl.when(needed(k))
            def _():
                load(k).wait()

    def visit(g, k, count, bound, own):
        keys = kv[k, pl.ds(g * rows, count * BLOCK), :]
        score = lax.dot_general(keys, query_ref[0, g], NT, preferred_element_type=F32)
        key_at = lax.broadcasted_iota(jnp.int32, (BLOCK, columns), 0)
        if own:
            limit = lax.broadcasted_iota(jnp.int32, (BLOCK, columns), 1) % BLOCK
            allowed = key_at <= limit
        else:
            allowed = key_at < bound - (count - 1) * BLOCK
        last = jnp.where(allowed, score[(count - 1) * BLOCK :], -1e30)
        if count > 1:
            score = jnp.concatenate([score[: (count - 1) * BLOCK], last], axis=0)
        else:
            score = last
        best = jnp.max(score, axis=0, keepdims=True)
        if not own:
            before = top[...]
            best = jnp.maximum(best, before)
            fade = jnp.exp2((before - best) * factor)
        weights = jnp.exp2((score - best) * factor)
        added = jnp.sum(weights, axis=0, keepdims=True)
        base = kv_heads * rows + g * HEAD_DIM
        stack = [
            kv[k, pl.ds(base + c * kv_heads * HEAD_DIM, HEAD_DIM), :] for c in range(count)
        ]
        turned = stack[0] if count == 1 else jnp.concatenate(stack, axis=1)
        product = jnp.dot(turned, weights.astype(BF16), preferred_element_type=F32)
        top[...] = best
        if own:
            total[...] = added
            state[...] = product
        else:
            total[...] = total[...] * fade + added
            state[...] = state[...] * fade + product

    for g in range(kv_heads):
        for count in range(1, chunks + 1):
            @pl.when(block == count - 1)
            def _():
                visit(g, 0, count, None, True)

        def other(k, carry):
            @pl.when(needed(k))
            def _():
                bound = info_ref[2 + lax.bitwise_xor(me, k)]
                for count in range(1, chunks + 1):
                    low, high = (count - 1) * BLOCK, count * BLOCK
                    @pl.when((bound > low) & (bound <= high))
                    def _():
                        visit(g, k, count, bound, False)

            return carry

        lax.fori_loop(1, shards, other, 0)
        result = state[...] / total[...]
        for h in range(group):
            at = (g * group + h) * HEAD_DIM
            rows_sc[:, at : at + HEAD_DIM] = jnp.transpose(
                result[:, h * BLOCK : (h + 1) * BLOCK]
            ).astype(BF16)

    @pl.when(pl.program_id(0) == 0)
    def _():
        load_weight.wait()

    width = outs[0].shape[1]
    for part in range(parts):
        owner = lax.rem(info_ref[1] + part, parts)
        span = pl.ds(pl.multiple_of(owner * width, width), width)
        outs[part][...] = jnp.dot(
            rows_sc[...], weight[:, span], preferred_element_type=F32
        ).astype(BF16)


def finish(pieces, tp_ref, aux_ref, hidden_ref, *refs):
    sums = refs[: 3 * pieces]
    out_ref, spread = refs[3 * pieces :]
    rows = aux_ref.shape[0]
    seq = hidden_ref.shape[0]

    @pl.when(pl.program_id(0) == 0)
    def _():
        local = jnp.transpose(aux_ref[:, 2 * HEAD_DIM : 3 * HEAD_DIM])[:1, :]
        place = lax.broadcasted_iota(jnp.int32, (seq, rows), 0)
        spread[...] = jnp.where(place == local.astype(jnp.int32), 1.0, 0.0).astype(BF16)

    parts = []
    for i in range(pieces):
        own, right, left = (ref[...].astype(F32) for ref in sums[3 * i : 3 * i + 3])
        parts.append(own + right + left)
    proj = parts[0] if pieces == 1 else jnp.concatenate(parts, axis=0)
    router = aux_ref[:, 3 * HEAD_DIM :][:, :1]
    update = proj * router
    high = update.astype(BF16)
    low = (update - high.astype(F32)).astype(BF16)
    change = jnp.dot(spread[...], high, preferred_element_type=F32)
    change = change + jnp.dot(spread[...], low, preferred_element_type=F32)
    out_ref[...] = (hidden_ref[...].astype(F32) + change).astype(BF16)


def params(megabytes, **more):
    return pltpu.CompilerParams(vmem_limit_bytes=megabytes << 20, **more)


def per_device(
    shards,
    parts,
    hidden,
    norm_gain,
    w_query,
    w_key,
    w_value,
    w_output,
    positions,
    counts,
    router_weight,
):
    seq, depth = hidden.shape
    rows = positions.shape[0]
    kv_heads = w_key.shape[1] // HEAD_DIM
    heads = w_query.shape[1] // HEAD_DIM
    group = heads // kv_heads
    width = w_output.shape[1] // parts
    me = lax.axis_index("ctx").astype(jnp.int32)
    tp = lax.axis_index("tp").astype(jnp.int32)
    smem = pl.BlockSpec(memory_space=pltpu.SMEM)
    anywhere = pl.BlockSpec(memory_space=pl.ANY)

    every_count = lax.all_gather(counts, "ctx", axis=0)
    info = jnp.concatenate(
        [me.reshape(1), tp.reshape(1), jnp.sum(every_count, axis=1).astype(jnp.int32)]
    )

    tile = 512
    payload_rows = 2 * kv_heads * rows

    def full(shape):
        return pl.BlockSpec(shape, lambda i: (0,) * len(shape))

    payload, normed, aux = pl.pallas_call(
        prepare,
        grid=(depth // tile,),
        in_specs=[
            smem,
            smem,
            full((1, rows)),
            full((1, HEAD_DIM)),
            full((1, depth)),
            full((1, seq)),
            pl.BlockSpec((seq, tile), lambda i: (0, i)),
            anywhere,
            anywhere,
        ],
        out_specs=[
            full((payload_rows, HEAD_DIM)),
            full((rows, depth)),
            full((rows, 4 * HEAD_DIM)),
        ],
        out_shape=[
            jax.ShapeDtypeStruct((payload_rows, HEAD_DIM), BF16),
            jax.ShapeDtypeStruct((rows, depth), BF16),
            jax.ShapeDtypeStruct((rows, 4 * HEAD_DIM), F32),
        ],
        scratch_shapes=[
            pltpu.VMEM((rows, seq), BF16),
            pltpu.VMEM((rows, 1), F32),
            pltpu.VMEM(w_key.shape, BF16),
            pltpu.VMEM(w_value.shape, BF16),
            pltpu.SemaphoreType.DMA((2,)),
        ],
        compiler_params=params(48),
        cost_estimate=pl.CostEstimate(
            flops=2 * rows * seq * depth, bytes_accessed=20 << 20, transcendentals=0
        ),
        name="prepare",
    )(
        counts,
        (me * seq).reshape(1),
        positions.reshape(1, rows),
        jnp.asarray(freq_rows()),
        norm_gain.reshape(1, depth),
        router_weight.reshape(1, seq),
        hidden,
        w_key,
        w_value,
    )

    def shift(value, mask, up_only=True):
        pairs = [(i, i ^ mask) for i in range(shards) if not up_only or i < i ^ mask]
        return lax.ppermute(value, "ctx", pairs)

    payloads = [payload, shift(payload, 1)] + [None] * (shards - 2)
    for mask in range(shards - 2, 0, -2):
        payloads[mask] = shift(payload, mask)
        payloads[mask + 1] = shift(payloads[mask], 1, up_only=False)

    per_step = 2 if group % 2 == 0 else 1
    query = pl.pallas_call(
        project_queries,
        grid=(heads // per_step,),
        in_specs=[
            full((rows, depth)),
            pl.BlockSpec((depth, per_step * HEAD_DIM), lambda i: (0, i)),
            full((rows, 4 * HEAD_DIM)),
        ],
        out_specs=pl.BlockSpec(
            (rows // BLOCK, 1, per_step * BLOCK, HEAD_DIM),
            lambda i: (0, i // (group // per_step), i % (group // per_step), 0),
        ),
        out_shape=jax.ShapeDtypeStruct(
            (rows // BLOCK, kv_heads, group * BLOCK, HEAD_DIM), BF16
        ),
        compiler_params=params(32),
        cost_estimate=pl.CostEstimate(
            flops=2 * rows * depth * w_query.shape[1], bytes_accessed=13 << 20, transcendentals=0
        ),
        name="queries",
    )(normed, w_query, aux)

    pieces = 2 if (rows // BLOCK) % 2 == 0 else 1
    piece_blocks = rows // BLOCK // pieces
    sums = []
    for piece in range(pieces):
        first = piece * piece_blocks
        outs = pl.pallas_call(
            functools.partial(attend, shards, parts, first),
            grid=(piece_blocks,),
            in_specs=[
                smem,
                pl.BlockSpec(
                    (1, kv_heads, group * BLOCK, HEAD_DIM),
                    lambda i, first=first: (first + i, 0, 0, 0),
                ),
            ]
            + [anywhere] * (shards + 1),
            out_specs=[pl.BlockSpec((BLOCK, width), lambda i: (i, 0))] * parts,
            out_shape=[jax.ShapeDtypeStruct((piece_blocks * BLOCK, width), BF16)] * parts,
            scratch_shapes=[
                pltpu.VMEM((shards, payload_rows, HEAD_DIM), BF16),
                pltpu.VMEM(w_output.shape, BF16),
                pltpu.VMEM((HEAD_DIM, group * BLOCK), F32),
                pltpu.VMEM((1, group * BLOCK), F32),
                pltpu.VMEM((1, group * BLOCK), F32),
                pltpu.VMEM((BLOCK, heads * HEAD_DIM), BF16),
                pltpu.SemaphoreType.DMA((shards,)),
                pltpu.SemaphoreType.DMA,
            ],
            compiler_params=params(40),
            cost_estimate=pl.CostEstimate(
                flops=8 << 30, bytes_accessed=14 << 20, transcendentals=8 << 20
            ),
            name=f"attend_{piece}",
        )(info, query, *payloads, w_output)
        right = left = None
        for step in range(1, parts):
            send_right = outs[parts - step]
            send_left = outs[step]
            if step > 1:
                send_right = send_right + right
                send_left = send_left + left
            right = lax.ppermute(send_right, "tp", [(t, t + 1) for t in range(step)])
            left = lax.ppermute(
                send_left, "tp", [(t, t - 1) for t in range(parts - step, parts)]
            )
        sums += [outs[0], right, left]

    column = 256
    piece_spec = pl.BlockSpec((piece_blocks * BLOCK, column), lambda i, tp_ref: (0, i))
    return pl.pallas_call(
        functools.partial(finish, pieces),
        grid_spec=pltpu.PrefetchScalarGridSpec(
            num_scalar_prefetch=1,
            grid=(width // column,),
            in_specs=[
                pl.BlockSpec((rows, 4 * HEAD_DIM), lambda i, tp_ref: (0, 0)),
                pl.BlockSpec(
                    (seq, column), lambda i, tp_ref: (0, tp_ref[0] * (width // column) + i)
                ),
            ]
            + [piece_spec] * (3 * pieces),
            out_specs=pl.BlockSpec((seq, column), lambda i, tp_ref: (0, i)),
            scratch_shapes=[pltpu.VMEM((seq, rows), BF16)],
        ),
        out_shape=jax.ShapeDtypeStruct((seq, width), BF16),
        compiler_params=params(32),
        name="finish",
    )(tp.reshape(1), aux, hidden, *sums)


def solution(mesh):
    shards, parts = mesh.shape["ctx"], mesh.shape["tp"]
    return jax.shard_map(
        functools.partial(per_device, shards, parts),
        mesh=mesh,
        in_specs=(
            P("ctx", None),
            P(),
            P(None, "tp"),
            P(None, "tp"),
            P(None, "tp"),
            P("tp", None),
            P("ctx"),
            P("ctx"),
            P("ctx"),
        ),
        out_specs=P("ctx", "tp"),
        check_vma=False,
    )
```

```python
import functools

import jax
import jax.numpy as jnp
import numpy as np
from jax import lax
from jax.experimental import pallas as pl
from jax.experimental.pallas import tpu as pltpu
from jax.sharding import PartitionSpec as P

HEAD_DIM = 128
BLOCK = 128
HEADER = 16
F32 = jnp.float32
BF16 = jnp.bfloat16
NT = (((1,), (1,)), ((), ()))


def freq_rows():
    half = HEAD_DIM // 2
    freq = 500000.0 ** (-2.0 * np.arange(half, dtype=np.float64) / HEAD_DIM)
    return np.concatenate([freq, freq]).astype(np.float32).reshape(1, HEAD_DIM)


def rope(field, cosine, sine):
    return field * cosine + pltpu.roll(field, HEAD_DIM // 2, 1) * sine


def prepare(
    counts_ref,
    base_ref,
    pos_ref,
    freq_ref,
    gain_ref,
    router_ref,
    hidden_ref,
    key_ref,
    value_ref,
    payload_ref,
    picked_ref,
    aux_ref,
    select,
    square,
    key_sum,
    value_sum,
):
    step = pl.program_id(0)
    rows = picked_ref.shape[0]
    seq = hidden_ref.shape[0]
    blocks = counts_ref.shape[0]
    tile = hidden_ref.shape[1]
    depth = tile * pl.num_programs(0)
    live = counts_ref[0]
    for b in range(1, blocks):
        live = live + counts_ref[b]

    @pl.when(step == 0)
    def _():
        slot = lax.broadcasted_iota(jnp.int32, (1, rows), 1)
        compact = jnp.full((1, rows), -1, jnp.int32)
        offset = jnp.int32(0)
        for b in range(blocks):
            count = counts_ref[b]
            inside = (slot >= b * BLOCK) & (slot < b * BLOCK + count)
            compact = jnp.where(inside, slot - b * BLOCK + offset, compact)
            offset = offset + count
        position = pos_ref[...].astype(F32)
        band = 64
        sign = jnp.where(
            lax.broadcasted_iota(jnp.int32, (1, HEAD_DIM), 1) < HEAD_DIM // 2, -1.0, 1.0
        )

        @pl.loop(0, rows // band)
        def _(i):
            span = pl.ds(pl.multiple_of(i * band, band), band)
            line = lax.broadcasted_iota(jnp.int32, (band, rows), 0) + i * band
            pos_col = jnp.sum(jnp.where(line == compact, position, 0.0), axis=1, keepdims=True)
            line = lax.broadcasted_iota(jnp.int32, (band, 1), 0) + i * band
            local = jnp.where(line < live, pos_col.astype(jnp.int32) - base_ref[0], -1)
            hit = lax.broadcasted_iota(jnp.int32, (band, seq), 1) == local
            select[span, :] = jnp.where(hit, 1.0, 0.0).astype(BF16)
            router = jnp.sum(jnp.where(hit, router_ref[...], 0.0), axis=1, keepdims=True)
            angle = pos_col * freq_ref[...]
            shape = (band, HEAD_DIM)
            aux_ref[span, :HEAD_DIM] = jnp.cos(angle)
            aux_ref[span, HEAD_DIM : 2 * HEAD_DIM] = jnp.sin(angle) * sign
            aux_ref[span, 2 * HEAD_DIM : 3 * HEAD_DIM] = jnp.broadcast_to(
                local.astype(F32), shape
            )
            aux_ref[span, 3 * HEAD_DIM : 4 * HEAD_DIM] = jnp.broadcast_to(router, shape)

        square[...] = jnp.zeros_like(square)
        key_sum[...] = jnp.zeros_like(key_sum)
        value_sum[...] = jnp.zeros_like(value_sum)

    field = jnp.dot(select[...], hidden_ref[...], preferred_element_type=F32)
    power = field * field
    total = power[:, :HEAD_DIM]
    for i in range(1, tile // HEAD_DIM):
        total = total + power[:, i * HEAD_DIM : (i + 1) * HEAD_DIM]
    square[...] += total
    field = (field * gain_ref[...]).astype(BF16)
    picked_ref[...] = field
    key_sum[...] += jnp.dot(field, key_ref[...], preferred_element_type=F32)
    value_sum[...] += jnp.dot(field, value_ref[...], preferred_element_type=F32)

    @pl.when(step == pl.num_programs(0) - 1)
    def _():
        kv_heads = key_ref.shape[1] // HEAD_DIM

        @pl.loop(0, rows // BLOCK)
        def _(c):
            span = pl.ds(pl.multiple_of(c * BLOCK, BLOCK), BLOCK)
            mean = jnp.sum(square[span, :], axis=1, keepdims=True) / depth
            scale = jnp.broadcast_to(lax.rsqrt(mean + 1e-05), (BLOCK, HEAD_DIM))
            aux_ref[span, 4 * HEAD_DIM :] = scale
            cosine = aux_ref[span, :HEAD_DIM]
            sine = aux_ref[span, HEAD_DIM : 2 * HEAD_DIM]
            for g in range(kv_heads):
                head = slice(g * HEAD_DIM, (g + 1) * HEAD_DIM)
                turned = rope(key_sum[span, head] * scale, cosine, sine)
                at = pl.multiple_of((2 * c * kv_heads + g) * BLOCK, BLOCK)
                payload_ref[pl.ds(at, BLOCK), :] = jnp.transpose(turned).astype(BF16)
                at = pl.multiple_of((2 * c * kv_heads + kv_heads + g) * BLOCK, BLOCK)
                payload_ref[pl.ds(at, BLOCK), :] = (value_sum[span, head] * scale).astype(BF16)

        half = lax.broadcasted_iota(jnp.int32, (HEADER, HEAD_DIM), 1) < HEAD_DIM // 2
        digits = jnp.where(half, live // HEADER, lax.rem(live, HEADER))
        payload_ref[2 * kv_heads * rows :, :] = digits.astype(F32).astype(BF16)


def project_queries(picked_ref, weight_ref, aux_ref, out_ref):
    rows = picked_ref.shape[0]
    factor = HEAD_DIM**-0.5 * 1.4426950408889634
    fields = jnp.dot(picked_ref[...], weight_ref[...], preferred_element_type=F32)
    cosine = aux_ref[:, :HEAD_DIM]
    sine = aux_ref[:, HEAD_DIM : 2 * HEAD_DIM]
    scale = aux_ref[:, 4 * HEAD_DIM :] * factor
    for h in range(weight_ref.shape[1] // HEAD_DIM):
        turned = rope(fields[:, h * HEAD_DIM : (h + 1) * HEAD_DIM] * scale, cosine, sine)
        turned = turned.astype(BF16)
        for r in range(rows // BLOCK):
            out_ref[r, 0, h * BLOCK : (h + 1) * BLOCK, :] = turned[r * BLOCK : (r + 1) * BLOCK]


def attend(shards, parts, first_block, blocks, info_ref, query_ref, *refs):
    payloads = refs[:shards]
    output_hbm = refs[shards]
    outs = refs[shards + 1 : shards + 1 + parts]
    kv, weight, scores, tops, state, rows_sc, place, bound, sems, weight_sem = refs[
        shards + 1 + parts :
    ]
    me = info_ref[0]
    kv_heads = query_ref.shape[1]
    group = query_ref.shape[2] // BLOCK
    columns = blocks * group * BLOCK
    height = 2 * kv_heads * BLOCK
    chunks = kv.shape[1] // height
    load_weight = pltpu.make_async_copy(output_hbm, weight, weight_sem)

    def each_copy(act):
        for k in range(shards):
            def run():
                act(pltpu.make_async_copy(payloads[k], kv.at[k], sems.at[k]))

            if k == 0:
                run()
            else:
                pl.when(lax.bitwise_xor(me, k) < me)(run)

    each_copy(lambda copy: copy.start())
    load_weight.start()
    each_copy(lambda copy: copy.wait())

    half = lax.broadcasted_iota(jnp.int32, (HEADER, BLOCK), 1) < BLOCK // 2
    at = jnp.int32(0)
    for k in range(1, shards):
        digits = kv[k, chunks * height :, :].astype(F32)
        high = jnp.max(jnp.where(half, digits, 0.0)).astype(jnp.int32)
        low = jnp.max(jnp.where(half, 0.0, digits)).astype(jnp.int32)
        live = jnp.where(lax.bitwise_xor(me, k) < me, high * HEADER + low, 0)
        for c in range(chunks):
            @pl.when(live > c * BLOCK)
            def _():
                place[at + c] = k * chunks + c
                bound[at + c] = jnp.minimum(live - c * BLOCK, BLOCK)

        at = at + (live + BLOCK - 1) // BLOCK
    for c in range(first_block + blocks):
        place[at + c] = c
        bound[at + c] = BLOCK

    limit = at + first_block
    lane = lax.broadcasted_iota(jnp.int32, (1, BLOCK), 1)
    ones = jnp.ones((BLOCK, BLOCK), BF16)
    wide = 4
    def rows_of(i, piece):
        spot = place[i]
        start = pl.multiple_of((spot % chunks) * height + piece * BLOCK, BLOCK)
        return kv[spot // chunks, pl.ds(start, BLOCK), :]

    def keys(g, first, count):
        parts_ = [rows_of(first + u, g) for u in range(count)]
        return parts_[0] if count == 1 else jnp.concatenate(parts_, axis=1)

    def values(g, first, count):
        parts_ = [
            jnp.concatenate([rows_of(first + u, kv_heads + g), ones], axis=1)
            for u in range(count)
        ]
        return parts_[0] if count == 1 else jnp.concatenate(parts_, axis=0)

    def column(first, count):
        return pl.ds(pl.multiple_of((blocks + first) * BLOCK, BLOCK), count * BLOCK)

    row = lax.broadcasted_iota(jnp.int32, (columns, BLOCK), 0)
    row = row // (group * BLOCK) * BLOCK + row % BLOCK
    slot = lax.broadcasted_iota(jnp.int32, (columns, BLOCK), 1)
    whole = limit // wide

    together = tops.shape[0]

    @pl.loop(0, kv_heads // together)
    def _(turn):
        heads = [turn * together + u for u in range(together)]
        queries = [
            jnp.concatenate([query_ref[first_block + b, g] for b in range(blocks)], axis=0)
            for g in heads
        ]

        def score(first, count):
            for a, g in enumerate(heads):
                value = jnp.dot(queries[a], keys(g, first, count), preferred_element_type=F32)
                best = tops[a]
                for u in range(count):
                    bias = jnp.where(lane < bound[first + u], 0.0, -1e30)
                    part = value[:, u * BLOCK : (u + 1) * BLOCK] + bias
                    scores[a, :, column(first + u, 1)] = part
                    best = jnp.maximum(best, part)
                tops[a] = best

        def gather(first, at, count):
            for a, g in enumerate(heads):
                top = jnp.concatenate([tops[a]] * count, axis=1)
                weights = jnp.exp2(scores[a, :, column(at, count)] - top).astype(BF16)
                state[a] += jnp.dot(
                    weights, values(g, first, count), preferred_element_type=F32
                )

        tops[...] = jnp.full_like(tops, -1e30)
        state[...] = jnp.zeros_like(state)
        for a, g in enumerate(heads):
            for b in range(blocks):
                own = jnp.dot(queries[a], keys(g, limit + b, 1), preferred_element_type=F32)
                own = jnp.where(slot + b * BLOCK <= row, own, -1e30)
                scores[a, :, b * BLOCK : (b + 1) * BLOCK] = own
                tops[a] = jnp.maximum(tops[a], own)

        @pl.loop(0, whole)
        def _(i):
            score(i * wide, wide)

        @pl.loop(whole * wide, limit)
        def _(i):
            score(i, 1)

        for a in range(together):
            top = jnp.max(tops[a], axis=1, keepdims=True)
            tops[a] = jnp.broadcast_to(top, (columns, BLOCK))

        @pl.loop(0, whole)
        def _(i):
            gather(i * wide, i * wide, wide)

        @pl.loop(whole * wide, limit + blocks)
        def _(i):
            gather(i, jnp.where(i < limit, i, i - limit - blocks), 1)

        for a, g in enumerate(heads):
            result = (state[a, :, :BLOCK] / state[a, :, BLOCK:]).astype(BF16)
            for b in range(blocks):
                for h in range(group):
                    at = (g * group + h) * HEAD_DIM
                    start = (b * group + h) * BLOCK
                    rows_sc[
                        b * BLOCK : (b + 1) * BLOCK,
                        pl.ds(pl.multiple_of(at, HEAD_DIM), HEAD_DIM),
                    ] = result[start : start + BLOCK]

    load_weight.wait()
    width = outs[0].shape[1]
    tile = 256
    for part in range(parts):
        owner = lax.rem(info_ref[1] + part, parts)

        @pl.loop(0, width // tile)
        def _(i):
            span = pl.ds(pl.multiple_of(owner * width + i * tile, tile), tile)
            into = pl.ds(pl.multiple_of(i * tile, tile), tile)
            outs[part][:, into] = jnp.dot(
                rows_sc[...], weight[:, span], preferred_element_type=F32
            ).astype(BF16)


def finish(pieces, tp_ref, aux_ref, hidden_ref, *refs):
    sums = refs[: 3 * pieces]
    out_ref, spread = refs[3 * pieces :]
    rows = aux_ref.shape[0]
    seq = hidden_ref.shape[0]

    @pl.when(pl.program_id(0) == 0)
    def _():
        local = jnp.transpose(aux_ref[:, 2 * HEAD_DIM : 3 * HEAD_DIM])[:1, :]
        place = lax.broadcasted_iota(jnp.int32, (seq, rows), 0)
        spread[...] = jnp.where(place == local.astype(jnp.int32), 1.0, 0.0).astype(BF16)

    parts = []
    for i in range(pieces):
        own, right, left = (ref[...].astype(F32) for ref in sums[3 * i : 3 * i + 3])
        parts.append(own + right + left)
    proj = parts[0] if pieces == 1 else jnp.concatenate(parts, axis=0)
    router = aux_ref[:, 3 * HEAD_DIM : 3 * HEAD_DIM + 1]
    update = proj * router
    high = update.astype(BF16)
    low = (update - high.astype(F32)).astype(BF16)
    change = jnp.dot(spread[...], high, preferred_element_type=F32)
    change = change + jnp.dot(spread[...], low, preferred_element_type=F32)
    out_ref[...] = (hidden_ref[...].astype(F32) + change).astype(BF16)


def params(megabytes, **more):
    return pltpu.CompilerParams(vmem_limit_bytes=megabytes << 20, **more)


def per_device(
    shards,
    parts,
    hidden,
    norm_gain,
    w_query,
    w_key,
    w_value,
    w_output,
    positions,
    counts,
    router_weight,
):
    seq, depth = hidden.shape
    rows = positions.shape[0]
    kv_heads = w_key.shape[1] // HEAD_DIM
    heads = w_query.shape[1] // HEAD_DIM
    group = heads // kv_heads
    width = w_output.shape[1] // parts
    me = lax.axis_index("ctx").astype(jnp.int32)
    tp = lax.axis_index("tp").astype(jnp.int32)
    smem = pl.BlockSpec(memory_space=pltpu.SMEM)
    anywhere = pl.BlockSpec(memory_space=pl.ANY)

    info = jnp.stack([me, tp])

    tile = 512
    payload_rows = 2 * kv_heads * rows + HEADER

    def full(shape):
        return pl.BlockSpec(shape, lambda i: (0,) * len(shape))

    payload, picked, aux = pl.pallas_call(
        prepare,
        grid=(depth // tile,),
        in_specs=[
            smem,
            smem,
            full((1, rows)),
            full((1, HEAD_DIM)),
            pl.BlockSpec((1, tile), lambda i: (0, i)),
            full((1, seq)),
            pl.BlockSpec((seq, tile), lambda i: (0, i)),
            pl.BlockSpec((tile, w_key.shape[1]), lambda i: (i, 0)),
            pl.BlockSpec((tile, w_value.shape[1]), lambda i: (i, 0)),
        ],
        out_specs=[
            full((payload_rows, HEAD_DIM)),
            pl.BlockSpec((rows, tile), lambda i: (0, i)),
            full((rows, 5 * HEAD_DIM)),
        ],
        out_shape=[
            jax.ShapeDtypeStruct((payload_rows, HEAD_DIM), BF16),
            jax.ShapeDtypeStruct((rows, depth), BF16),
            jax.ShapeDtypeStruct((rows, 5 * HEAD_DIM), F32),
        ],
        scratch_shapes=[
            pltpu.VMEM((rows, seq), BF16),
            pltpu.VMEM((rows, HEAD_DIM), F32),
            pltpu.VMEM((rows, w_key.shape[1]), F32),
            pltpu.VMEM((rows, w_value.shape[1]), F32),
        ],
        compiler_params=params(60),
        cost_estimate=pl.CostEstimate(
            flops=2 * rows * seq * depth, bytes_accessed=20 << 20, transcendentals=0
        ),
        name="prepare",
    )(
        counts,
        (me * seq).reshape(1),
        positions.reshape(1, rows),
        jnp.asarray(freq_rows()),
        norm_gain.reshape(1, depth),
        router_weight.reshape(1, seq),
        hidden,
        w_key,
        w_value,
    )

    def shift(value, mask, up_only=True):
        pairs = [(i, i ^ mask) for i in range(shards) if not up_only or i < i ^ mask]
        return lax.ppermute(value, "ctx", pairs)

    payloads = [payload] + [None] * (shards - 1)
    far = range(shards - 2, 0, -2)
    for mask in far:
        payloads[mask] = shift(payload, mask)
    payloads[1] = shift(payload, 1)

    per_step = 2 if group % 2 == 0 else 1
    query = pl.pallas_call(
        project_queries,
        grid=(heads // per_step,),
        in_specs=[
            full((rows, depth)),
            pl.BlockSpec((depth, per_step * HEAD_DIM), lambda i: (0, i)),
            full((rows, 5 * HEAD_DIM)),
        ],
        out_specs=pl.BlockSpec(
            (rows // BLOCK, 1, per_step * BLOCK, HEAD_DIM),
            lambda i: (0, i // (group // per_step), i % (group // per_step), 0),
        ),
        out_shape=jax.ShapeDtypeStruct(
            (rows // BLOCK, kv_heads, group * BLOCK, HEAD_DIM), BF16
        ),
        compiler_params=params(60),
        cost_estimate=pl.CostEstimate(
            flops=2 * rows * depth * w_query.shape[1], bytes_accessed=13 << 20, transcendentals=0
        ),
        name="queries",
    )(picked, w_query, aux)

    held = lax.optimization_barrier((query, *(payloads[mask] for mask in far)))
    query = held[0]
    for mask, value in zip(far, held[1:]):
        payloads[mask] = value
        payloads[mask + 1] = shift(value, 1, up_only=False)

    def hop(step, products, carried):
        right, left = products[parts - step], products[step]
        if step > 1:
            right, left = right + carried[0], left + carried[1]
        return (
            lax.ppermute(right, "tp", [(t, t + 1) for t in range(step)]),
            lax.ppermute(left, "tp", [(t, t - 1) for t in range(parts - step, parts)]),
        )

    def rest(plan, info, tp_ref, query, aux, hidden, w_output, *payloads):
        made, carried = [], []
        first = 0
        for blocks in plan:
            columns = blocks * group * BLOCK
            together = kv_heads if blocks == 1 else 1
            outs = pl.pallas_call(
                functools.partial(attend, shards, parts, first, blocks),
                grid=(1,),
                in_specs=[smem, full(query.shape)] + [anywhere] * (shards + 1),
                out_specs=[full((blocks * BLOCK, width))] * parts,
                out_shape=[jax.ShapeDtypeStruct((blocks * BLOCK, width), BF16)] * parts,
                scratch_shapes=[
                    pltpu.VMEM((shards, payload_rows, HEAD_DIM), BF16),
                    pltpu.VMEM(w_output.shape, BF16),
                    pltpu.VMEM((together, columns, shards * rows), F32),
                    pltpu.VMEM((together, columns, BLOCK), F32),
                    pltpu.VMEM((together, columns, 2 * BLOCK), F32),
                    pltpu.VMEM((blocks * BLOCK, heads * HEAD_DIM), BF16),
                    pltpu.SMEM((shards * (rows // BLOCK),), jnp.int32),
                    pltpu.SMEM((shards * (rows // BLOCK),), jnp.int32),
                    pltpu.SemaphoreType.DMA((shards,)),
                    pltpu.SemaphoreType.DMA,
                ],
                compiler_params=params(60),
                cost_estimate=pl.CostEstimate(
                    flops=8 << 30, bytes_accessed=14 << 20, transcendentals=8 << 20
                ),
                name=f"attend_{first}_{blocks}",
            )(info, query, *payloads, w_output)
            if made:
                carried[0], outs = lax.optimization_barrier((carried[0], outs))
            made.append(outs)
            carried.append(hop(1, outs, None))
            first += blocks
            info, outs = lax.optimization_barrier((info, outs))
            made[-1] = outs
        for step in range(2, parts):
            carried = [hop(step, outs, moved) for outs, moved in zip(made, carried)]
        sums = []
        for outs, moved in zip(made, carried):
            sums += [outs[0], *moved]

        here = first * BLOCK
        column = 256
        specs = []
        for blocks in plan:
            spec = pl.BlockSpec((blocks * BLOCK, column), lambda i, tp_ref: (0, i))
            specs += [spec] * 3
        return pl.pallas_call(
            functools.partial(finish, len(plan)),
            grid_spec=pltpu.PrefetchScalarGridSpec(
                num_scalar_prefetch=1,
                grid=(width // column,),
                in_specs=[
                    pl.BlockSpec((here, 5 * HEAD_DIM), lambda i, tp_ref: (0, 0)),
                    pl.BlockSpec(
                        (seq, column), lambda i, tp_ref: (0, tp_ref[0] * (width // column) + i)
                    ),
                ]
                + specs,
                out_specs=pl.BlockSpec((seq, column), lambda i, tp_ref: (0, i)),
                scratch_shapes=[pltpu.VMEM((seq, here), BF16)],
            ),
            out_shape=jax.ShapeDtypeStruct((seq, width), BF16),
            compiler_params=params(60),
            name=f"finish_{first}",
        )(tp_ref, aux, hidden, *sums)

    plans = [(1,), (2,)] + [(n // 2, n - n // 2) for n in range(3, rows // BLOCK + 1)]
    used = (jnp.sum(counts) - 1) // BLOCK
    return lax.switch(
        used,
        [functools.partial(rest, plan) for plan in plans],
        info,
        tp.reshape(1),
        query,
        aux,
        hidden,
        w_output,
        *payloads,
    )


def solution(mesh):
    shards, parts = mesh.shape["ctx"], mesh.shape["tp"]
    return jax.shard_map(
        functools.partial(per_device, shards, parts),
        mesh=mesh,
        in_specs=(
            P("ctx", None),
            P(),
            P(None, "tp"),
            P(None, "tp"),
            P(None, "tp"),
            P("tp", None),
            P("ctx"),
            P("ctx"),
            P("ctx"),
        ),
        out_specs=P("ctx", "tp"),
        check_vma=False,
    )
```

```python
import functools

import jax
import jax.numpy as jnp
import numpy as np
from jax import lax
from jax.experimental import pallas as pl
from jax.experimental.pallas import tpu as pltpu
from jax.sharding import PartitionSpec as P

HEAD_DIM = 128
BLOCK = 128
HEADER = 16
F32 = jnp.float32
BF16 = jnp.bfloat16
NT = (((1,), (1,)), ((), ()))


def freq_rows():
    half = HEAD_DIM // 2
    freq = 500000.0 ** (-2.0 * np.arange(half, dtype=np.float64) / HEAD_DIM)
    return np.concatenate([freq, freq]).astype(np.float32).reshape(1, HEAD_DIM)


def rope(field, cosine, sine):
    return field * cosine + pltpu.roll(field, HEAD_DIM // 2, 1) * sine


def prepare(
    counts_ref,
    base_ref,
    pos_ref,
    freq_ref,
    gain_ref,
    router_ref,
    hidden_ref,
    key_ref,
    value_ref,
    payload_ref,
    picked_ref,
    aux_ref,
    select,
    square,
    key_sum,
    value_sum,
):
    step = pl.program_id(0)
    rows = picked_ref.shape[0]
    seq = hidden_ref.shape[0]
    blocks = counts_ref.shape[0]
    tile = hidden_ref.shape[1]
    depth = tile * pl.num_programs(0)
    live = counts_ref[0]
    for b in range(1, blocks):
        live = live + counts_ref[b]

    @pl.when(step == 0)
    def _():
        slot = lax.broadcasted_iota(jnp.int32, (1, rows), 1)
        compact = jnp.full((1, rows), -1, jnp.int32)
        offset = jnp.int32(0)
        for b in range(blocks):
            count = counts_ref[b]
            inside = (slot >= b * BLOCK) & (slot < b * BLOCK + count)
            compact = jnp.where(inside, slot - b * BLOCK + offset, compact)
            offset = offset + count
        position = pos_ref[...].astype(F32)
        band = 64

        @pl.loop(0, rows // band)
        def _(i):
            span = pl.ds(pl.multiple_of(i * band, band), band)
            line = lax.broadcasted_iota(jnp.int32, (band, rows), 0) + i * band
            pos_col = jnp.sum(jnp.where(line == compact, position, 0.0), axis=1, keepdims=True)
            line = lax.broadcasted_iota(jnp.int32, (band, 1), 0) + i * band
            local = jnp.where(line < live, pos_col.astype(jnp.int32) - base_ref[0], -1)
            hit = lax.broadcasted_iota(jnp.int32, (band, seq), 1) == local
            select[span, :] = jnp.where(hit, 1.0, 0.0).astype(BF16)
            router = jnp.sum(jnp.where(hit, router_ref[...], 0.0), axis=1, keepdims=True)
            shape = (band, HEAD_DIM)
            aux_ref[span, 4 * HEAD_DIM :] = jnp.broadcast_to(pos_col, shape)
            aux_ref[span, 2 * HEAD_DIM : 3 * HEAD_DIM] = jnp.broadcast_to(
                local.astype(F32), shape
            )
            aux_ref[span, 3 * HEAD_DIM : 4 * HEAD_DIM] = jnp.broadcast_to(router, shape)

        square[...] = jnp.zeros_like(square)
        key_sum[...] = jnp.zeros_like(key_sum)
        value_sum[...] = jnp.zeros_like(value_sum)

    share = rows // (depth // tile)
    span = pl.ds(pl.multiple_of(step * share, share), share)
    angle = aux_ref[span, 4 * HEAD_DIM :] * freq_ref[...]
    first = lax.broadcasted_iota(jnp.int32, (1, HEAD_DIM), 1) < HEAD_DIM // 2
    aux_ref[span, :HEAD_DIM] = jnp.cos(angle)
    aux_ref[span, HEAD_DIM : 2 * HEAD_DIM] = jnp.sin(angle) * jnp.where(first, -1.0, 1.0)
    field = jnp.dot(select[...], hidden_ref[...], preferred_element_type=F32)
    power = field * field
    total = power[:, :HEAD_DIM]
    for i in range(1, tile // HEAD_DIM):
        total = total + power[:, i * HEAD_DIM : (i + 1) * HEAD_DIM]
    square[...] += total
    field = (field * gain_ref[...]).astype(BF16)
    picked_ref[...] = field
    key_sum[...] += jnp.dot(field, key_ref[...], preferred_element_type=F32)
    value_sum[...] += jnp.dot(field, value_ref[...], preferred_element_type=F32)

    @pl.when(step == pl.num_programs(0) - 1)
    def _():
        kv_heads = key_ref.shape[1] // HEAD_DIM

        @pl.loop(0, rows // BLOCK)
        def _(c):
            span = pl.ds(pl.multiple_of(c * BLOCK, BLOCK), BLOCK)
            mean = jnp.sum(square[span, :], axis=1, keepdims=True) / depth
            scale = jnp.broadcast_to(lax.rsqrt(mean + 1e-05), (BLOCK, HEAD_DIM))
            aux_ref[span, 4 * HEAD_DIM :] = scale
            cosine = aux_ref[span, :HEAD_DIM]
            sine = aux_ref[span, HEAD_DIM : 2 * HEAD_DIM]
            for g in range(kv_heads):
                head = slice(g * HEAD_DIM, (g + 1) * HEAD_DIM)
                turned = rope(key_sum[span, head] * scale, cosine, sine)
                at = pl.multiple_of((2 * c * kv_heads + g) * BLOCK, BLOCK)
                payload_ref[pl.ds(at, BLOCK), :] = jnp.transpose(turned).astype(BF16)
                at = pl.multiple_of((2 * c * kv_heads + kv_heads + g) * BLOCK, BLOCK)
                payload_ref[pl.ds(at, BLOCK), :] = (value_sum[span, head] * scale).astype(BF16)

        half = lax.broadcasted_iota(jnp.int32, (HEADER, HEAD_DIM), 1) < HEAD_DIM // 2
        digits = jnp.where(half, live // HEADER, lax.rem(live, HEADER))
        payload_ref[2 * kv_heads * rows :, :] = digits.astype(F32).astype(BF16)


def project_queries(picked_ref, weight_ref, aux_ref, out_ref):
    rows = picked_ref.shape[0]
    factor = HEAD_DIM**-0.5 * 1.4426950408889634
    fields = jnp.dot(picked_ref[...], weight_ref[...], preferred_element_type=F32)
    cosine = aux_ref[:, :HEAD_DIM]
    sine = aux_ref[:, HEAD_DIM : 2 * HEAD_DIM]
    scale = aux_ref[:, 4 * HEAD_DIM :] * factor
    for h in range(weight_ref.shape[1] // HEAD_DIM):
        turned = rope(fields[:, h * HEAD_DIM : (h + 1) * HEAD_DIM] * scale, cosine, sine)
        turned = turned.astype(BF16)
        for r in range(rows // BLOCK):
            out_ref[r, 0, h * BLOCK : (h + 1) * BLOCK, :] = turned[r * BLOCK : (r + 1) * BLOCK]


def attend(shards, parts, first_block, cuts, info_ref, query_ref, *refs):
    payloads = refs[:shards]
    output_hbm = refs[shards]
    blocks = sum(cuts)
    each = 1 + parts // 2
    outs = refs[shards + 1 : shards + 1 + len(cuts) * each]
    kv, weight, scores, tops, state, rows_sc, place, bound, sems, weight_sem = refs[
        shards + 1 + len(cuts) * each :
    ]
    me = info_ref[0]
    kv_heads = query_ref.shape[1]
    group = query_ref.shape[2] // BLOCK
    columns = blocks * group * BLOCK
    height = 2 * kv_heads * BLOCK
    chunks = kv.shape[1] // height
    load_weight = pltpu.make_async_copy(output_hbm, weight, weight_sem)

    def each_copy(act):
        for k in range(shards):
            def run():
                act(pltpu.make_async_copy(payloads[k], kv.at[k], sems.at[k]))

            if k == 0:
                run()
            else:
                pl.when(lax.bitwise_xor(me, k) < me)(run)

    each_copy(lambda copy: copy.start())
    load_weight.start()
    each_copy(lambda copy: copy.wait())

    half = lax.broadcasted_iota(jnp.int32, (HEADER, BLOCK), 1) < BLOCK // 2
    at = jnp.int32(0)
    for k in range(1, shards):
        digits = kv[k, chunks * height :, :].astype(F32)
        high = jnp.max(jnp.where(half, digits, 0.0)).astype(jnp.int32)
        low = jnp.max(jnp.where(half, 0.0, digits)).astype(jnp.int32)
        live = jnp.where(lax.bitwise_xor(me, k) < me, high * HEADER + low, 0)
        for c in range(chunks):
            @pl.when(live > c * BLOCK)
            def _():
                place[at + c] = k * chunks + c
                bound[at + c] = jnp.minimum(live - c * BLOCK, BLOCK)

        at = at + (live + BLOCK - 1) // BLOCK
    for c in range(first_block):
        place[at + c] = c
        bound[at + c] = BLOCK
    limit = at + first_block
    wide = 4
    for c in range(2 * wide):
        place[limit + c] = 0
        bound[limit + c] = 0
    groups = (limit + blocks + wide - 1) // wide
    lane = lax.broadcasted_iota(jnp.int32, (1, BLOCK), 1)
    ones = jnp.ones((BLOCK, BLOCK), BF16)

    def rows_of(spot, piece):
        start = pl.multiple_of((spot % chunks) * height + piece * BLOCK, BLOCK)
        return kv[spot // chunks, pl.ds(start, BLOCK), :]

    def column(first, count):
        return pl.ds(pl.multiple_of(first * BLOCK, BLOCK), count * BLOCK)

    row = lax.broadcasted_iota(jnp.int32, (columns, BLOCK), 0)
    row = row // (group * BLOCK) * BLOCK + row % BLOCK
    slot = lax.broadcasted_iota(jnp.int32, (columns, BLOCK), 1)
    together = tops.shape[0]

    @pl.loop(0, kv_heads // together)
    def _(turn):
        heads = [turn * together + u for u in range(together)]
        queries = [
            jnp.concatenate([query_ref[first_block + b, g] for b in range(blocks)], axis=0)
            for g in heads
        ]
        for a, g in enumerate(heads):
            best = None
            for b in range(blocks):
                keys = rows_of(first_block + b, g)
                own = jnp.dot(queries[a], keys, preferred_element_type=F32)
                own = jnp.where(slot + b * BLOCK <= row, own, -1e30)
                scores[a, :, b * BLOCK : (b + 1) * BLOCK] = own
                best = own if b == 0 else jnp.maximum(best, own)
            tops[a] = best
        state[...] = jnp.zeros_like(state)

        @pl.loop(0, (groups * wide - blocks + wide - 1) // wide)
        def _(i):
            first = i * wide
            for a, g in enumerate(heads):
                keys = [rows_of(place[first + u], g) for u in range(wide)]
                keys = jnp.concatenate(keys, axis=1)
                value = jnp.dot(queries[a], keys, preferred_element_type=F32)
                best = tops[a]
                for u in range(wide):
                    bias = jnp.where(lane < bound[first + u], 0.0, -1e30)
                    part = value[:, u * BLOCK : (u + 1) * BLOCK] + bias
                    scores[a, :, column(blocks + first + u, 1)] = part
                    best = jnp.maximum(best, part)
                tops[a] = best

        for a in range(together):
            top = jnp.max(tops[a], axis=1, keepdims=True)
            tops[a] = jnp.broadcast_to(top, (columns, BLOCK))

        @pl.loop(0, groups)
        def _(i):
            for a, g in enumerate(heads):
                values = []
                for u in range(wide):
                    at = i * wide + u - blocks
                    spot = jnp.where(at < 0, first_block + blocks + at, place[jnp.maximum(at, 0)])
                    values.append(jnp.concatenate([rows_of(spot, kv_heads + g), ones], axis=1))
                top = jnp.concatenate([tops[a]] * wide, axis=1)
                weights = jnp.exp2(scores[a, :, column(i * wide, wide)] - top).astype(BF16)
                state[a] += jnp.dot(
                    weights, jnp.concatenate(values, axis=0), preferred_element_type=F32
                )

        for a, g in enumerate(heads):
            result = (state[a, :, :BLOCK] / state[a, :, BLOCK:]).astype(BF16)
            for b in range(blocks):
                for h in range(group):
                    at = (g * group + h) * HEAD_DIM
                    start = (b * group + h) * BLOCK
                    rows_sc[
                        b * BLOCK : (b + 1) * BLOCK,
                        pl.ds(pl.multiple_of(at, HEAD_DIM), HEAD_DIM),
                    ] = result[start : start + BLOCK]

    load_weight.wait()
    width = outs[1].shape[1]
    for part in range(parts):
        owner = lax.bitwise_xor(info_ref[1], part)
        span = pl.ds(pl.multiple_of(owner * width, width), width)
        product = jnp.dot(rows_sc[...], weight[:, span], preferred_element_type=F32).astype(BF16)
        start = 0
        for u, cut in enumerate(cuts):
            high = cut * BLOCK
            piece = product[start : start + high]
            if part % 2:
                outs[u * each][part // 2 * high : (part // 2 + 1) * high, :] = piece
            else:
                outs[u * each + 1 + part // 2][...] = piece
            start += high


def finish(pieces, terms, tp_ref, aux_ref, hidden_ref, *refs):
    sums = refs[: terms * pieces]
    out_ref, spread = refs[terms * pieces :]
    rows = aux_ref.shape[0]
    seq = hidden_ref.shape[0]

    @pl.when(pl.program_id(0) == 0)
    def _():
        local = jnp.transpose(aux_ref[:, 2 * HEAD_DIM : 3 * HEAD_DIM])[:1, :]
        place = lax.broadcasted_iota(jnp.int32, (seq, rows), 0)
        spread[...] = jnp.where(place == local.astype(jnp.int32), 1.0, 0.0).astype(BF16)

    parts = []
    for i in range(pieces):
        total = sums[terms * i][...].astype(F32)
        for ref in sums[terms * i + 1 : terms * (i + 1)]:
            total = total + ref[...].astype(F32)
        parts.append(total)
    proj = parts[0] if pieces == 1 else jnp.concatenate(parts, axis=0)
    router = aux_ref[:, 3 * HEAD_DIM : 3 * HEAD_DIM + 1]
    update = proj * router
    high = update.astype(BF16)
    low = (update - high.astype(F32)).astype(BF16)
    change = jnp.dot(spread[...], high, preferred_element_type=F32)
    change = change + jnp.dot(spread[...], low, preferred_element_type=F32)
    out_ref[...] = (hidden_ref[...].astype(F32) + change).astype(BF16)


def params(megabytes, **more):
    return pltpu.CompilerParams(vmem_limit_bytes=megabytes << 20, **more)


def per_device(
    shards,
    parts,
    hidden,
    norm_gain,
    w_query,
    w_key,
    w_value,
    w_output,
    positions,
    counts,
    router_weight,
):
    seq, depth = hidden.shape
    rows = positions.shape[0]
    kv_heads = w_key.shape[1] // HEAD_DIM
    heads = w_query.shape[1] // HEAD_DIM
    group = heads // kv_heads
    width = w_output.shape[1] // parts
    me = lax.axis_index("ctx").astype(jnp.int32)
    tp = lax.axis_index("tp").astype(jnp.int32)
    smem = pl.BlockSpec(memory_space=pltpu.SMEM)
    anywhere = pl.BlockSpec(memory_space=pl.ANY)

    info = jnp.stack([me, tp])

    tile = 1024
    payload_rows = 2 * kv_heads * rows + HEADER

    def full(shape):
        return pl.BlockSpec(shape, lambda i: (0,) * len(shape))

    payload, picked, aux = pl.pallas_call(
        prepare,
        grid=(depth // tile,),
        in_specs=[
            smem,
            smem,
            full((1, rows)),
            full((1, HEAD_DIM)),
            pl.BlockSpec((1, tile), lambda i: (0, i)),
            full((1, seq)),
            pl.BlockSpec((seq, tile), lambda i: (0, i)),
            pl.BlockSpec((tile, w_key.shape[1]), lambda i: (i, 0)),
            pl.BlockSpec((tile, w_value.shape[1]), lambda i: (i, 0)),
        ],
        out_specs=[
            full((payload_rows, HEAD_DIM)),
            pl.BlockSpec((rows, tile), lambda i: (0, i)),
            full((rows, 5 * HEAD_DIM)),
        ],
        out_shape=[
            jax.ShapeDtypeStruct((payload_rows, HEAD_DIM), BF16),
            jax.ShapeDtypeStruct((rows, depth), BF16),
            jax.ShapeDtypeStruct((rows, 5 * HEAD_DIM), F32),
        ],
        scratch_shapes=[
            pltpu.VMEM((rows, seq), BF16),
            pltpu.VMEM((rows, HEAD_DIM), F32),
            pltpu.VMEM((rows, w_key.shape[1]), F32),
            pltpu.VMEM((rows, w_value.shape[1]), F32),
        ],
        compiler_params=params(60),
        cost_estimate=pl.CostEstimate(
            flops=2 * rows * seq * depth, bytes_accessed=20 << 20, transcendentals=0
        ),
        name="prepare",
    )(
        counts,
        (me * seq).reshape(1),
        positions.reshape(1, rows),
        jnp.asarray(freq_rows()),
        norm_gain.reshape(1, depth),
        router_weight.reshape(1, seq),
        hidden,
        w_key,
        w_value,
    )

    def shift(value, mask, up_only=True):
        pairs = [(i, i ^ mask) for i in range(shards) if not up_only or i < i ^ mask]
        return lax.ppermute(value, "ctx", pairs)

    payloads = [payload] + [None] * (shards - 1)
    far = range(shards - 2, 0, -2)
    for mask in far:
        payloads[mask] = shift(payload, mask)
    payloads[1] = shift(payload, 1)

    per_step = 2 if group % 2 == 0 else 1
    query = pl.pallas_call(
        project_queries,
        grid=(heads // per_step,),
        in_specs=[
            full((rows, depth)),
            pl.BlockSpec((depth, per_step * HEAD_DIM), lambda i: (0, i)),
            full((rows, 5 * HEAD_DIM)),
        ],
        out_specs=pl.BlockSpec(
            (rows // BLOCK, 1, per_step * BLOCK, HEAD_DIM),
            lambda i: (0, i // (group // per_step), i % (group // per_step), 0),
        ),
        out_shape=jax.ShapeDtypeStruct(
            (rows // BLOCK, kv_heads, group * BLOCK, HEAD_DIM), BF16
        ),
        compiler_params=params(60),
        cost_estimate=pl.CostEstimate(
            flops=2 * rows * depth * w_query.shape[1], bytes_accessed=13 << 20, transcendentals=0
        ),
        name="queries",
    )(picked, w_query, aux)

    held = lax.optimization_barrier((query, *(payloads[mask] for mask in far)))
    query = held[0]
    for mask, value in zip(far, held[1:]):
        payloads[mask] = value
        payloads[mask + 1] = shift(value, 1, up_only=False)

    def swap(value, mask):
        return lax.ppermute(value, "tp", [(t, t ^ mask) for t in range(parts)])

    each = 1 + parts // 2

    def attention(first, cuts, info, query, w_output, payloads):
        blocks = sum(cuts)
        columns = blocks * group * BLOCK
        together = kv_heads if blocks == 1 else 1
        shapes = []
        for cut in cuts:
            shapes += [(parts // 2 * cut * BLOCK, width)]
            shapes += [(cut * BLOCK, width)] * (parts // 2)
        slots = shards * (rows // BLOCK) + 8
        return pl.pallas_call(
            functools.partial(attend, shards, parts, first, cuts),
            grid=(1,),
            in_specs=[smem, full(query.shape)] + [anywhere] * (shards + 1),
            out_specs=[full(shape) for shape in shapes],
            out_shape=[jax.ShapeDtypeStruct(shape, BF16) for shape in shapes],
            scratch_shapes=[
                pltpu.VMEM((shards, payload_rows, HEAD_DIM), BF16),
                pltpu.VMEM(w_output.shape, BF16),
                pltpu.VMEM((together, columns, slots * BLOCK), F32),
                pltpu.VMEM((together, columns, BLOCK), F32),
                pltpu.VMEM((together, columns, 2 * BLOCK), F32),
                pltpu.VMEM((blocks * BLOCK, heads * HEAD_DIM), BF16),
                pltpu.SMEM((slots,), jnp.int32),
                pltpu.SMEM((slots,), jnp.int32),
                pltpu.SemaphoreType.DMA((shards,)),
                pltpu.SemaphoreType.DMA,
            ],
            compiler_params=params(60),
            cost_estimate=pl.CostEstimate(
                flops=8 << 30, bytes_accessed=14 << 20, transcendentals=8 << 20
            ),
            name=f"attend_{first}_{blocks}",
        )(info, query, *payloads, w_output)

    def halve(blocks, outs, came):
        high = blocks * BLOCK
        held = list(outs[1:])
        terms = [held[0], came]
        for j in range(1, len(held)):
            held[j] = held[j] + came[j * high : (j + 1) * high]
        mask = 2
        while mask < parts:
            step = mask // 2
            gone = range(step, len(held), 2 * step)
            came = swap(jnp.concatenate([held[j] for j in gone]), mask)
            terms.append(came)
            for i, j in enumerate(range(2 * step, len(held), 2 * step)):
                held[j] = held[j] + came[(i + 1) * high : (i + 2) * high]
            mask *= 2
        return terms

    def rest(plan, info, tp_ref, query, aux, hidden, w_output, outs, *payloads):
        made, sums = [], []
        pieces = [cut for cuts in plan for cut in cuts]
        first = 0
        for cuts in plan:
            if first:
                if len(made) > 1:
                    info, made[-2][1] = lax.optimization_barrier((info, made[-2][1]))
                outs = attention(first, cuts, info, query, w_output, payloads)
            info, outs = lax.optimization_barrier((info, outs))
            for u in range(len(cuts)):
                made.append([outs[u * each : (u + 1) * each], swap(outs[u * each], 1), None])
            if len(made) > 2:
                made[-3][2] = halve(pieces[len(made) - 3], *made[-3][:2])
            first += sum(cuts)
        for piece, (outs, came, terms) in enumerate(made):
            sums += terms or halve(pieces[piece], outs, came)

        terms = len(sums) // len(pieces)
        here = first * BLOCK
        column = 256
        specs = []
        for blocks in pieces:
            spec = pl.BlockSpec((blocks * BLOCK, column), lambda i, tp_ref: (0, i))
            specs += [spec] * terms
        return pl.pallas_call(
            functools.partial(finish, len(pieces), terms),
            grid_spec=pltpu.PrefetchScalarGridSpec(
                num_scalar_prefetch=1,
                grid=(width // column,),
                in_specs=[
                    pl.BlockSpec((here, 5 * HEAD_DIM), lambda i, tp_ref: (0, 0)),
                    pl.BlockSpec(
                        (seq, column), lambda i, tp_ref: (0, tp_ref[0] * (width // column) + i)
                    ),
                ]
                + specs,
                out_specs=pl.BlockSpec((seq, column), lambda i, tp_ref: (0, i)),
                scratch_shapes=[pltpu.VMEM((seq, here), BF16)],
            ),
            out_shape=jax.ShapeDtypeStruct((seq, width), BF16),
            compiler_params=params(63),
            name=f"finish_{first}",
        )(tp_ref, aux, hidden, *sums)

    plans = [((1,),) * n for n in range(1, rows // BLOCK + 1)]
    used = (jnp.sum(counts) - 1) // BLOCK
    return lax.switch(
        used,
        [functools.partial(rest, plan) for plan in plans],
        info,
        tp.reshape(1),
        query,
        aux,
        hidden,
        w_output,
        attention(0, (1,), info, query, w_output, payloads),
        *payloads,
    )


def solution(mesh):
    shards, parts = mesh.shape["ctx"], mesh.shape["tp"]
    return jax.shard_map(
        functools.partial(per_device, shards, parts),
        mesh=mesh,
        in_specs=(
            P("ctx", None),
            P(),
            P(None, "tp"),
            P(None, "tp"),
            P(None, "tp"),
            P("tp", None),
            P("ctx"),
            P("ctx"),
            P("ctx"),
        ),
        out_specs=P("ctx", "tp"),
        check_vma=False,
    )
```

```python
import functools

import jax
import jax.numpy as jnp
import numpy as np
from jax import lax
from jax.experimental import pallas as pl
from jax.experimental.pallas import tpu as pltpu
from jax.sharding import PartitionSpec as P

HEAD_DIM = 128
BLOCK = 128
HEADER = 16
F32 = jnp.float32
BF16 = jnp.bfloat16
NT = (((1,), (1,)), ((), ()))


def freq_rows():
    half = HEAD_DIM // 2
    freq = 500000.0 ** (-2.0 * np.arange(half, dtype=np.float64) / HEAD_DIM)
    return np.concatenate([freq, freq]).astype(np.float32).reshape(1, HEAD_DIM)


def rope(field, cosine, sine):
    return field * cosine + pltpu.roll(field, HEAD_DIM // 2, 1) * sine


def prepare(
    counts_ref,
    base_ref,
    pos_ref,
    freq_ref,
    gain_ref,
    router_ref,
    hidden_ref,
    key_ref,
    value_ref,
    payload_ref,
    picked_ref,
    aux_ref,
    select,
    square,
    key_sum,
    value_sum,
):
    step = pl.program_id(0)
    rows = picked_ref.shape[0]
    seq = hidden_ref.shape[0]
    blocks = counts_ref.shape[0]
    tile = hidden_ref.shape[1]
    depth = tile * pl.num_programs(0)
    live = counts_ref[0]
    for b in range(1, blocks):
        live = live + counts_ref[b]

    @pl.when(step == 0)
    def _():
        slot = lax.broadcasted_iota(jnp.int32, (1, rows), 1)
        compact = jnp.full((1, rows), -1, jnp.int32)
        offset = jnp.int32(0)
        for b in range(blocks):
            count = counts_ref[b]
            inside = (slot >= b * BLOCK) & (slot < b * BLOCK + count)
            compact = jnp.where(inside, slot - b * BLOCK + offset, compact)
            offset = offset + count
        position = pos_ref[...].astype(F32)
        band = 64

        @pl.loop(0, rows // band)
        def _(i):
            span = pl.ds(pl.multiple_of(i * band, band), band)
            line = lax.broadcasted_iota(jnp.int32, (band, rows), 0) + i * band
            pos_col = jnp.sum(jnp.where(line == compact, position, 0.0), axis=1, keepdims=True)
            line = lax.broadcasted_iota(jnp.int32, (band, 1), 0) + i * band
            local = jnp.where(line < live, pos_col.astype(jnp.int32) - base_ref[0], -1)
            hit = lax.broadcasted_iota(jnp.int32, (band, seq), 1) == local
            select[span, :] = jnp.where(hit, 1.0, 0.0).astype(BF16)
            router = jnp.sum(jnp.where(hit, router_ref[...], 0.0), axis=1, keepdims=True)
            shape = (band, HEAD_DIM)
            aux_ref[span, 4 * HEAD_DIM :] = jnp.broadcast_to(pos_col, shape)
            aux_ref[span, 2 * HEAD_DIM : 3 * HEAD_DIM] = jnp.broadcast_to(
                local.astype(F32), shape
            )
            aux_ref[span, 3 * HEAD_DIM : 4 * HEAD_DIM] = jnp.broadcast_to(router, shape)

        square[...] = jnp.zeros_like(square)
        key_sum[...] = jnp.zeros_like(key_sum)
        value_sum[...] = jnp.zeros_like(value_sum)

    share = rows // (depth // tile)
    span = pl.ds(pl.multiple_of(step * share, share), share)
    angle = aux_ref[span, 4 * HEAD_DIM :] * freq_ref[...]
    first = lax.broadcasted_iota(jnp.int32, (1, HEAD_DIM), 1) < HEAD_DIM // 2
    aux_ref[span, :HEAD_DIM] = jnp.cos(angle)
    aux_ref[span, HEAD_DIM : 2 * HEAD_DIM] = jnp.sin(angle) * jnp.where(first, -1.0, 1.0)
    field = jnp.dot(select[...], hidden_ref[...], preferred_element_type=F32)
    power = field * field
    total = power[:, :HEAD_DIM]
    for i in range(1, tile // HEAD_DIM):
        total = total + power[:, i * HEAD_DIM : (i + 1) * HEAD_DIM]
    square[...] += total
    field = (field * gain_ref[...]).astype(BF16)
    picked_ref[...] = field
    key_sum[...] += jnp.dot(field, key_ref[...], preferred_element_type=F32)
    value_sum[...] += jnp.dot(field, value_ref[...], preferred_element_type=F32)

    @pl.when(step == pl.num_programs(0) - 1)
    def _():
        kv_heads = key_ref.shape[1] // HEAD_DIM

        @pl.loop(0, rows // BLOCK)
        def _(c):
            span = pl.ds(pl.multiple_of(c * BLOCK, BLOCK), BLOCK)
            mean = jnp.sum(square[span, :], axis=1, keepdims=True) / depth
            scale = jnp.broadcast_to(lax.rsqrt(mean + 1e-05), (BLOCK, HEAD_DIM))
            aux_ref[span, 4 * HEAD_DIM :] = scale
            cosine = aux_ref[span, :HEAD_DIM]
            sine = aux_ref[span, HEAD_DIM : 2 * HEAD_DIM]
            for g in range(kv_heads):
                head = slice(g * HEAD_DIM, (g + 1) * HEAD_DIM)
                turned = rope(key_sum[span, head] * scale, cosine, sine)
                at = pl.multiple_of((2 * c * kv_heads + g) * BLOCK, BLOCK)
                payload_ref[pl.ds(at, BLOCK), :] = jnp.transpose(turned).astype(BF16)
                at = pl.multiple_of((2 * c * kv_heads + kv_heads + g) * BLOCK, BLOCK)
                payload_ref[pl.ds(at, BLOCK), :] = (value_sum[span, head] * scale).astype(BF16)

        half = lax.broadcasted_iota(jnp.int32, (HEADER, HEAD_DIM), 1) < HEAD_DIM // 2
        digits = jnp.where(half, live // HEADER, lax.rem(live, HEADER))
        payload_ref[2 * kv_heads * rows :, :] = digits.astype(F32).astype(BF16)


def project_queries(picked_ref, weight_ref, aux_ref, out_ref):
    rows = picked_ref.shape[0]
    factor = HEAD_DIM**-0.5 * 1.4426950408889634
    fields = jnp.dot(picked_ref[...], weight_ref[...], preferred_element_type=F32)
    cosine = aux_ref[:, :HEAD_DIM]
    sine = aux_ref[:, HEAD_DIM : 2 * HEAD_DIM]
    scale = aux_ref[:, 4 * HEAD_DIM :] * factor
    for h in range(weight_ref.shape[1] // HEAD_DIM):
        turned = rope(fields[:, h * HEAD_DIM : (h + 1) * HEAD_DIM] * scale, cosine, sine)
        turned = turned.astype(BF16)
        for r in range(rows // BLOCK):
            out_ref[r, 0, h * BLOCK : (h + 1) * BLOCK, :] = turned[r * BLOCK : (r + 1) * BLOCK]


def attend(shards, parts, first_block, cuts, info_ref, query_ref, *refs):
    payloads = refs[:shards]
    output_hbm = refs[shards]
    blocks = sum(cuts)
    each = 1 + parts // 2
    outs = refs[shards + 1 : shards + 1 + len(cuts) * each]
    kv, weight, scores, tops, state, rows_sc, place, bound, sems, weight_sem = refs[
        shards + 1 + len(cuts) * each :
    ]
    me = info_ref[0]
    kv_heads = query_ref.shape[1]
    group = query_ref.shape[2] // BLOCK
    columns = blocks * group * BLOCK
    height = 2 * kv_heads * BLOCK
    chunks = kv.shape[1] // height
    load_weight = pltpu.make_async_copy(output_hbm, weight, weight_sem)

    def each_copy(act):
        for k in range(shards):
            def run():
                act(pltpu.make_async_copy(payloads[k], kv.at[k], sems.at[k]))

            if k == 0:
                run()
            else:
                pl.when(lax.bitwise_xor(me, k) < me)(run)

    each_copy(lambda copy: copy.start())
    load_weight.start()
    each_copy(lambda copy: copy.wait())

    half = lax.broadcasted_iota(jnp.int32, (HEADER, BLOCK), 1) < BLOCK // 2
    at = jnp.int32(0)
    for k in range(1, shards):
        digits = kv[k, chunks * height :, :].astype(F32)
        high = jnp.max(jnp.where(half, digits, 0.0)).astype(jnp.int32)
        low = jnp.max(jnp.where(half, 0.0, digits)).astype(jnp.int32)
        live = jnp.where(lax.bitwise_xor(me, k) < me, high * HEADER + low, 0)
        for c in range(chunks):
            @pl.when(live > c * BLOCK)
            def _():
                place[at + c] = k * chunks + c
                bound[at + c] = jnp.minimum(live - c * BLOCK, BLOCK)

        at = at + (live + BLOCK - 1) // BLOCK
    for c in range(first_block):
        place[at + c] = c
        bound[at + c] = BLOCK
    limit = at + first_block
    wide = 4
    for c in range(2 * wide):
        place[limit + c] = 0
        bound[limit + c] = 0
    groups = (limit + blocks + wide - 1) // wide
    lane = lax.broadcasted_iota(jnp.int32, (1, BLOCK), 1)
    ones = jnp.ones((BLOCK, BLOCK), BF16)

    def rows_of(spot, piece):
        start = pl.multiple_of((spot % chunks) * height + piece * BLOCK, BLOCK)
        return kv[spot // chunks, pl.ds(start, BLOCK), :]

    def column(first, count):
        return pl.ds(pl.multiple_of(first * BLOCK, BLOCK), count * BLOCK)

    row = lax.broadcasted_iota(jnp.int32, (columns, BLOCK), 0)
    row = row // (group * BLOCK) * BLOCK + row % BLOCK
    slot = lax.broadcasted_iota(jnp.int32, (columns, BLOCK), 1)
    together = tops.shape[0]

    @pl.loop(0, kv_heads // together)
    def _(turn):
        heads = [turn * together + u for u in range(together)]
        queries = [
            jnp.concatenate([query_ref[first_block + b, g] for b in range(blocks)], axis=0)
            for g in heads
        ]
        for a, g in enumerate(heads):
            best = None
            for b in range(blocks):
                keys = rows_of(first_block + b, g)
                own = jnp.dot(queries[a], keys, preferred_element_type=F32)
                own = jnp.where(slot + b * BLOCK <= row, own, -1e30)
                scores[a, :, b * BLOCK : (b + 1) * BLOCK] = own
                best = own if b == 0 else jnp.maximum(best, own)
            tops[a] = best
        state[...] = jnp.zeros_like(state)

        @pl.loop(0, (groups * wide - blocks + wide - 1) // wide)
        def _(i):
            first = i * wide
            for a, g in enumerate(heads):
                keys = [rows_of(place[first + u], g) for u in range(wide)]
                keys = jnp.concatenate(keys, axis=1)
                value = jnp.dot(queries[a], keys, preferred_element_type=F32)
                best = tops[a]
                for u in range(wide):
                    bias = jnp.where(lane < bound[first + u], 0.0, -1e30)
                    part = value[:, u * BLOCK : (u + 1) * BLOCK] + bias
                    scores[a, :, column(blocks + first + u, 1)] = part
                    best = jnp.maximum(best, part)
                tops[a] = best

        for a in range(together):
            top = jnp.max(tops[a], axis=1, keepdims=True)
            tops[a] = jnp.broadcast_to(top, (columns, BLOCK))

        @pl.loop(0, groups)
        def _(i):
            for a, g in enumerate(heads):
                values = []
                for u in range(wide):
                    at = i * wide + u - blocks
                    spot = jnp.where(at < 0, first_block + blocks + at, place[jnp.maximum(at, 0)])
                    values.append(jnp.concatenate([rows_of(spot, kv_heads + g), ones], axis=1))
                top = jnp.concatenate([tops[a]] * wide, axis=1)
                weights = jnp.exp2(scores[a, :, column(i * wide, wide)] - top).astype(BF16)
                state[a] += jnp.dot(
                    weights, jnp.concatenate(values, axis=0), preferred_element_type=F32
                )

        for a, g in enumerate(heads):
            result = (state[a, :, :BLOCK] / state[a, :, BLOCK:]).astype(BF16)
            for b in range(blocks):
                for h in range(group):
                    at = (g * group + h) * HEAD_DIM
                    start = (b * group + h) * BLOCK
                    rows_sc[
                        b * BLOCK : (b + 1) * BLOCK,
                        pl.ds(pl.multiple_of(at, HEAD_DIM), HEAD_DIM),
                    ] = result[start : start + BLOCK]

    load_weight.wait()
    width = outs[1].shape[1]
    for part in range(parts):
        owner = lax.bitwise_xor(info_ref[1], part)
        span = pl.ds(pl.multiple_of(owner * width, width), width)
        product = jnp.dot(rows_sc[...], weight[:, span], preferred_element_type=F32).astype(BF16)
        start = 0
        for u, cut in enumerate(cuts):
            high = cut * BLOCK
            piece = product[start : start + high]
            if part % 2:
                outs[u * each][part // 2 * high : (part // 2 + 1) * high, :] = piece
            else:
                outs[u * each + 1 + part // 2][...] = piece
            start += high


def finish(pieces, terms, tp_ref, aux_ref, hidden_ref, *refs):
    sums = refs[: terms * pieces]
    out_ref, spread = refs[terms * pieces :]
    rows = aux_ref.shape[0]
    seq = hidden_ref.shape[0]

    @pl.when(pl.program_id(0) == 0)
    def _():
        local = jnp.transpose(aux_ref[:, 2 * HEAD_DIM : 3 * HEAD_DIM])[:1, :]
        place = lax.broadcasted_iota(jnp.int32, (seq, rows), 0)
        spread[...] = jnp.where(place == local.astype(jnp.int32), 1.0, 0.0).astype(BF16)

    parts = []
    for i in range(pieces):
        total = sums[terms * i][...].astype(F32)
        for ref in sums[terms * i + 1 : terms * (i + 1)]:
            total = total + ref[...].astype(F32)
        parts.append(total)
    proj = parts[0] if pieces == 1 else jnp.concatenate(parts, axis=0)
    router = aux_ref[:, 3 * HEAD_DIM : 3 * HEAD_DIM + 1]
    update = proj * router
    change = jnp.dot(spread[...], update.astype(BF16), preferred_element_type=F32)
    out_ref[...] = (hidden_ref[...].astype(F32) + change).astype(BF16)


def params(megabytes, **more):
    return pltpu.CompilerParams(vmem_limit_bytes=megabytes << 20, **more)


def per_device(
    shards,
    parts,
    hidden,
    norm_gain,
    w_query,
    w_key,
    w_value,
    w_output,
    positions,
    counts,
    router_weight,
):
    seq, depth = hidden.shape
    rows = positions.shape[0]
    kv_heads = w_key.shape[1] // HEAD_DIM
    heads = w_query.shape[1] // HEAD_DIM
    group = heads // kv_heads
    width = w_output.shape[1] // parts
    me = lax.axis_index("ctx").astype(jnp.int32)
    tp = lax.axis_index("tp").astype(jnp.int32)
    smem = pl.BlockSpec(memory_space=pltpu.SMEM)
    anywhere = pl.BlockSpec(memory_space=pl.ANY)

    info = jnp.stack([me, tp])

    tile = 1024
    payload_rows = 2 * kv_heads * rows + HEADER

    def full(shape):
        return pl.BlockSpec(shape, lambda i: (0,) * len(shape))

    payload, picked, aux = pl.pallas_call(
        prepare,
        grid=(depth // tile,),
        in_specs=[
            smem,
            smem,
            full((1, rows)),
            full((1, HEAD_DIM)),
            pl.BlockSpec((1, tile), lambda i: (0, i)),
            full((1, seq)),
            pl.BlockSpec((seq, tile), lambda i: (0, i)),
            pl.BlockSpec((tile, w_key.shape[1]), lambda i: (i, 0)),
            pl.BlockSpec((tile, w_value.shape[1]), lambda i: (i, 0)),
        ],
        out_specs=[
            full((payload_rows, HEAD_DIM)),
            pl.BlockSpec((rows, tile), lambda i: (0, i)),
            full((rows, 5 * HEAD_DIM)),
        ],
        out_shape=[
            jax.ShapeDtypeStruct((payload_rows, HEAD_DIM), BF16),
            jax.ShapeDtypeStruct((rows, depth), BF16),
            jax.ShapeDtypeStruct((rows, 5 * HEAD_DIM), F32),
        ],
        scratch_shapes=[
            pltpu.VMEM((rows, seq), BF16),
            pltpu.VMEM((rows, HEAD_DIM), F32),
            pltpu.VMEM((rows, w_key.shape[1]), F32),
            pltpu.VMEM((rows, w_value.shape[1]), F32),
        ],
        compiler_params=params(60),
        cost_estimate=pl.CostEstimate(
            flops=2 * rows * seq * depth, bytes_accessed=20 << 20, transcendentals=0
        ),
        name="prepare",
    )(
        counts,
        (me * seq).reshape(1),
        positions.reshape(1, rows),
        jnp.asarray(freq_rows()),
        norm_gain.reshape(1, depth),
        router_weight.reshape(1, seq),
        hidden,
        w_key,
        w_value,
    )

    def shift(value, mask, up_only=True):
        pairs = [(i, i ^ mask) for i in range(shards) if not up_only or i < i ^ mask]
        return lax.ppermute(value, "ctx", pairs)

    payloads = [payload] + [None] * (shards - 1)
    far = range(shards - 2, 0, -2)
    for mask in far:
        payloads[mask] = shift(payload, mask)
    payloads[1] = shift(payload, 1)

    per_step = 2 if group % 2 == 0 else 1
    query = pl.pallas_call(
        project_queries,
        grid=(heads // per_step,),
        in_specs=[
            full((rows, depth)),
            pl.BlockSpec((depth, per_step * HEAD_DIM), lambda i: (0, i)),
            full((rows, 5 * HEAD_DIM)),
        ],
        out_specs=pl.BlockSpec(
            (rows // BLOCK, 1, per_step * BLOCK, HEAD_DIM),
            lambda i: (0, i // (group // per_step), i % (group // per_step), 0),
        ),
        out_shape=jax.ShapeDtypeStruct(
            (rows // BLOCK, kv_heads, group * BLOCK, HEAD_DIM), BF16
        ),
        compiler_params=params(60),
        cost_estimate=pl.CostEstimate(
            flops=2 * rows * depth * w_query.shape[1], bytes_accessed=13 << 20, transcendentals=0
        ),
        name="queries",
    )(picked, w_query, aux)

    used = (jnp.sum(counts) - 1) // BLOCK
    held = (query, info, used, *(payloads[mask] for mask in far))
    query, info, used, *held = lax.optimization_barrier(held)
    for mask, value in zip(far, held):
        payloads[mask] = value
        payloads[mask + 1] = shift(value, 1, up_only=False)

    def swap(value, mask):
        return lax.ppermute(value, "tp", [(t, t ^ mask) for t in range(parts)])

    each = 1 + parts // 2

    def attention(first, cuts, info, query, w_output, payloads):
        blocks = sum(cuts)
        columns = blocks * group * BLOCK
        together = kv_heads if blocks == 1 else 1
        shapes = []
        for cut in cuts:
            shapes += [(parts // 2 * cut * BLOCK, width)]
            shapes += [(cut * BLOCK, width)] * (parts // 2)
        slots = shards * (rows // BLOCK) + 8
        return pl.pallas_call(
            functools.partial(attend, shards, parts, first, cuts),
            grid=(1,),
            in_specs=[smem, full(query.shape)] + [anywhere] * (shards + 1),
            out_specs=[full(shape) for shape in shapes],
            out_shape=[jax.ShapeDtypeStruct(shape, BF16) for shape in shapes],
            scratch_shapes=[
                pltpu.VMEM((shards, payload_rows, HEAD_DIM), BF16),
                pltpu.VMEM(w_output.shape, BF16),
                pltpu.VMEM((together, columns, slots * BLOCK), F32),
                pltpu.VMEM((together, columns, BLOCK), F32),
                pltpu.VMEM((together, columns, 2 * BLOCK), F32),
                pltpu.VMEM((blocks * BLOCK, heads * HEAD_DIM), BF16),
                pltpu.SMEM((slots,), jnp.int32),
                pltpu.SMEM((slots,), jnp.int32),
                pltpu.SemaphoreType.DMA((shards,)),
                pltpu.SemaphoreType.DMA,
            ],
            compiler_params=params(60),
            cost_estimate=pl.CostEstimate(
                flops=1 << 20, bytes_accessed=1 << 18, transcendentals=0
            ),
            name=f"attend_{first}_{blocks}",
        )(info, query, *payloads, w_output)

    def halve(blocks, outs, came):
        high = blocks * BLOCK
        held = list(outs[1:])
        terms = [held[0], came]
        for j in range(1, len(held)):
            held[j] = held[j] + came[j * high : (j + 1) * high]
        mask = 2
        while mask < parts:
            step = mask // 2
            gone = range(step, len(held), 2 * step)
            came = swap(jnp.concatenate([held[j] for j in gone]), mask)
            terms.append(came)
            for i, j in enumerate(range(2 * step, len(held), 2 * step)):
                held[j] = held[j] + came[(i + 1) * high : (i + 2) * high]
            mask *= 2
        return terms

    def rest(plan, info, tp_ref, query, aux, hidden, w_output, outs, *payloads):
        made, sums = [], []
        pieces = [cut for cuts in plan for cut in cuts]
        first = 0
        for cuts in plan:
            if first:
                if len(made) > 1:
                    info, made[-2][1] = lax.optimization_barrier((info, made[-2][1]))
                    made[-2][2] = halve(pieces[len(made) - 2], *made[-2][:2])
                if len(made) > 2:
                    info, made[-3][2] = lax.optimization_barrier((info, made[-3][2]))
                outs = attention(first, cuts, info, query, w_output, payloads)
            info, outs = lax.optimization_barrier((info, outs))
            for u in range(len(cuts)):
                made.append([outs[u * each : (u + 1) * each], swap(outs[u * each], 1), None])
            first += sum(cuts)
        for piece, (outs, came, terms) in enumerate(made):
            sums += terms or halve(pieces[piece], outs, came)

        terms = len(sums) // len(pieces)
        here = first * BLOCK
        column = 256
        specs = []
        for blocks in pieces:
            spec = pl.BlockSpec((blocks * BLOCK, column), lambda i, tp_ref: (0, i))
            specs += [spec] * terms
        return pl.pallas_call(
            functools.partial(finish, len(pieces), terms),
            grid_spec=pltpu.PrefetchScalarGridSpec(
                num_scalar_prefetch=1,
                grid=(width // column,),
                in_specs=[
                    pl.BlockSpec((here, 5 * HEAD_DIM), lambda i, tp_ref: (0, 0)),
                    pl.BlockSpec(
                        (seq, column), lambda i, tp_ref: (0, tp_ref[0] * (width // column) + i)
                    ),
                ]
                + specs,
                out_specs=pl.BlockSpec((seq, column), lambda i, tp_ref: (0, i)),
                scratch_shapes=[pltpu.VMEM((seq, here), BF16)],
            ),
            out_shape=jax.ShapeDtypeStruct((seq, width), BF16),
            compiler_params=params(63),
            name=f"finish_{first}",
        )(tp_ref, aux, hidden, *sums)

    plans = [((1,),) * n for n in range(1, rows // BLOCK + 1)]
    return lax.switch(
        used,
        [functools.partial(rest, plan) for plan in plans],
        info,
        tp.reshape(1),
        query,
        aux,
        hidden,
        w_output,
        attention(0, (1,), info, query, w_output, payloads),
        *payloads,
    )


def solution(mesh):
    shards, parts = mesh.shape["ctx"], mesh.shape["tp"]
    return jax.shard_map(
        functools.partial(per_device, shards, parts),
        mesh=mesh,
        in_specs=(
            P("ctx", None),
            P(),
            P(None, "tp"),
            P(None, "tp"),
            P(None, "tp"),
            P("tp", None),
            P("ctx"),
            P("ctx"),
            P("ctx"),
        ),
        out_specs=P("ctx", "tp"),
        check_vma=False,
    )
```
